32 devices in a mesh: groups: 2 (over x), sensor: 16 (over z, y, core).
Axes of the slice: x: 2, y: 2, z: 4, core: 2. Of those that a mesh axis runs over, the one named last changes fastest.
Arguments:
- series: float32 [288, 1536], P(None, ('groups', 'sensor')), parts along dimension 1, may hold values from -6 to 6
- starts: int32 [2], P('groups'), parts along dimension 0, may hold values from 0 to 276
- sensor_order: int32 [1536], P(('groups', 'sensor')), parts along dimension 0, may hold values from 0 to 767, each once
- emb_src: float32 [10, 1536], P(None, ('groups', 'sensor')), parts along dimension 1, may hold values from -4.4 to 330
- emb_dst: float32 [10, 1536], P(None, ('groups', 'sensor')), parts along dimension 1, may hold values from -4.4 to 4.4
- start_proj: float32 [2, 32], replicated, may hold values from -4 to 4
- conv_weight: bfloat16 [64, 64], replicated, may hold values from -0.75 to 0.75
- mix_weight: bfloat16 [96, 32], replicated, may hold values from -0.625 to 0.625
- out_grad: bfloat16 [1536, 384], P(('groups', 'sensor')), parts along dimension 0, may hold values from -0.59765625 to 0.59765625
Outputs:
- layer_out: bfloat16 [1536, 384], P(('groups', 'sensor')), parts along dimension 0
- grad_src: float32 [10, 1536], P(None, ('groups', 'sensor')), parts along dimension 1
- grad_dst: float32 [10, 1536], P(None, ('groups', 'sensor')), parts along dimension 1
- grad_mix: float32 [192, 32], P('groups'), parts along dimension 0
The draws below stay inside these ranges and needn't reach their ends.
There are 2 independent parts, one for each index of `groups`. The reference program is written for one: setup_inputs(seed, part) draws one part's arguments, and reference() takes and returns one part's arrays. A program takes and returns all parts, laid end to end along the dimension named above; an argument that names none is the same for every part. Nothing has to cross between parts.
All inputs are finite; a program needn't handle non-finite values.
Results may differ from the reference program's by a relative error of at most 0.035.
Values may be sent and summed in bfloat16 or wider, within the bound.
A program may use at most 64 MiB of HBM per device.

```python
import math
import jax
import jax.numpy as jnp
from jax import lax

C = 32
EMB = 10
STEPS = 12
WIN = 1
TIME = 288
SENSORS = 768
FEAT = 384


def embedding_pair(key):
    keys = jax.random.split(jax.random.fold_in(key, 11), 5)
    dims = jnp.arange(EMB)[:, None]
    source = jax.random.truncated_normal(keys[0], -4.0, 4.0, (EMB, SENSORS), jnp.float32) * 0.816
    target = jax.random.truncated_normal(keys[1], -4.0, 4.0, (EMB, SENSORS), jnp.float32) * 0.816
    bulk_cols = jax.random.uniform(keys[2], (SENSORS,), jnp.float32) < 0.5
    bulk_level = jax.random.uniform(keys[3], (SENSORS,), jnp.float32, 1.5, 1.75)
    row_level = jax.random.uniform(keys[4], (SENSORS,), jnp.float32, 0.85, 1.15)
    target = jnp.where(bulk_cols[None, :], target * 0.1, target)
    source = jnp.where(dims == 1, row_level[None, :], source)
    target = jnp.where(dims == 1, jnp.where(bulk_cols[None, :], bulk_level[None, :], 0.0), target)
    return (source, target)


def draw_emb_src(key, part):
    return embedding_pair(key)[0]


def draw_emb_dst(key, part):
    return embedding_pair(key)[1]


def steps_of(own_key, shape, cuts, low, top_value):
    level = 1.0
    for dim, parts in cuts:
        heights = jax.random.uniform(jax.random.fold_in(jax.random.fold_in(own_key, 6), dim), (parts,), jnp.float32, low / len(cuts), top_value / len(cuts))
        level = level * jnp.repeat(jnp.exp(heights), shape[dim] // parts).reshape((-1,) + (1,) * (len(shape) - 1 - dim))
    return level


def gaussian(own_key, extent, spread, bound, cuts=(), kind=jnp.bfloat16):
    drawn = jax.random.normal(own_key, extent, jnp.float32) * spread
    if len(cuts) > 0:
        drawn = steps_of(own_key, extent, cuts, -0.22, 0.18) * drawn
    return jnp.clip(drawn, min=-bound, max=bound).astype(kind)


def setup_inputs(seed: int = 0, part: int = 0) -> dict:
    seeds = jax.random.split(jax.random.key(seed), 10)
    own_keys = jax.random.split(jax.random.fold_in(seeds[9], part), 10)
    return {
        "series": gaussian(own_keys[0], (TIME, SENSORS), 1.0, 6.0, ((1, 16),), jnp.float32),
        "starts": jax.random.randint(own_keys[1], (WIN,), 0, TIME - STEPS + 1).astype(jnp.int32),
        "sensor_order": jax.random.permutation(own_keys[2], SENSORS).astype(jnp.int32),
        "emb_src": draw_emb_src(jax.random.fold_in(jax.random.fold_in(seeds[9], part), 71), part),
        "emb_dst": draw_emb_dst(jax.random.fold_in(jax.random.fold_in(seeds[9], part), 71), part),
        "start_proj": gaussian(seeds[5], (2, C), 1.0, 4.0, (), jnp.float32),
        "conv_weight": gaussian(seeds[6], (2 * C, 2 * C), (2 * C) ** -0.5, 0.75),
        "mix_weight": gaussian(seeds[7], (3 * C, C), (3 * C) ** -0.5, 0.625),
        "out_grad": gaussian(own_keys[8], (SENSORS, FEAT), 0.1, 0.59765625, ((0, 16),)),
    }


highest = lax.Precision.HIGHEST

def front(readings, start_proj, conv_weight):
    sensors_here = readings.shape[0]
    channels = start_proj.shape[1]
    padded = jnp.concatenate([jnp.zeros(readings.shape[:-1] + (1,), jnp.float32), readings], axis=-1)
    inputs = (padded[..., None] * start_proj[0] + start_proj[1]).astype(jnp.bfloat16)
    paired = jnp.concatenate([inputs[:, :, :-1, :], inputs[:, :, 1:, :]], axis=-1).reshape(-1, 2 * channels)
    gate_terms = jnp.dot(paired, conv_weight, preferred_element_type=jnp.float32)
    hidden = (jnp.tanh(gate_terms[:, :channels]) * jax.nn.sigmoid(gate_terms[:, channels:])).astype(jnp.bfloat16)
    return (hidden.reshape(sensors_here, -1), inputs[:, :, 1:, :].reshape(sensors_here, -1))

def mixing(residual, hidden, diffused, second, mix_weight):
    channels = mix_weight.shape[1]
    stacked = jnp.concatenate([member.reshape(-1, channels) for member in (hidden, diffused, second)], axis=1)
    summed = residual.reshape(-1, channels).astype(jnp.float32) + jnp.dot(stacked, mix_weight, preferred_element_type=jnp.float32)
    return (summed.astype(jnp.bfloat16).reshape(hidden.shape[0], -1), stacked)

def channel_grads(out_grad, mix_weight):
    channels = mix_weight.shape[1]
    row_count = out_grad.shape[0]
    flat_grad = out_grad.reshape(-1, channels)
    dims = (((1,), (1,)), ((), ()))
    grad_once = lax.dot_general(flat_grad, mix_weight[channels:2 * channels], dims, preferred_element_type=jnp.float32)
    grad_twice = lax.dot_general(flat_grad, mix_weight[2 * channels:], dims, preferred_element_type=jnp.float32)
    return (grad_once.astype(jnp.bfloat16).reshape(row_count, -1), grad_twice.astype(jnp.bfloat16).reshape(row_count, -1))

def tile_probs(rows_emb, cols_emb, row_max, row_total):
    scores = jnp.einsum('ei,ej->ij', rows_emb, cols_emb, precision=highest)
    shares = jnp.exp(jnp.maximum(scores, 0.0) - row_max[:, None]) / row_total[:, None]
    return (scores, shares)

def pair_dot(left, right):
    return lax.dot_general(left, right, (((1,), (1,)), ((), ())), preferred_element_type=jnp.float32)

def reference(series, starts, sensor_order, emb_src, emb_dst, start_proj, conv_weight, mix_weight, out_grad):
    windows = jax.vmap(lambda first_step: lax.dynamic_slice_in_dim(series, first_step, STEPS, 0))(starts)
    readings = jnp.transpose(jnp.take(windows, sensor_order, axis=2), (2, 0, 1))
    hidden, residual = front(readings, start_proj, conv_weight)
    span_size = math.gcd(SENSORS, 512)
    blocks = jnp.arange(SENSORS // span_size, dtype=jnp.int32)

    def rows_of(values_in, position, axis_dim):
        return lax.dynamic_slice_in_dim(values_in, position * span_size, span_size, axis_dim)

    def stats_block(position):
        scores = jnp.maximum(jnp.einsum('ei,ej->ij', rows_of(emb_src, position, 1), emb_dst, precision=highest), 0.0)
        best_score = lax.optimization_barrier(jnp.max(scores, axis=1))
        return (best_score, lax.optimization_barrier(jnp.sum(jnp.exp(scores - best_score[:, None]), axis=1)))
    best_rows, total_rows = lax.map(stats_block, blocks)
    row_max = best_rows.reshape(-1)
    row_total = total_rows.reshape(-1)

    def apply_rows(features):

        def one_block(position):
            scores, shares = tile_probs(rows_of(emb_src, position, 1), emb_dst, rows_of(row_max, position, 0), rows_of(row_total, position, 0))
            return jnp.dot(shares.astype(jnp.bfloat16), features, preferred_element_type=jnp.float32)
        return lax.map(one_block, blocks).reshape(SENSORS, -1)
    diffused_full = apply_rows(hidden)
    diffused = diffused_full.astype(jnp.bfloat16)
    second_full = apply_rows(diffused)
    second = second_full.astype(jnp.bfloat16)
    layer_out, stacked = mixing(residual, hidden, diffused, second, mix_weight)
    grad_mix = lax.dot_general(stacked, out_grad.reshape(-1, C), (((0,), (0,)), ((), ())), preferred_element_type=jnp.float32)
    grad_once, grad_twice = channel_grads(out_grad, mix_weight)

    def back_block(position):
        scores, shares = tile_probs(emb_src, rows_of(emb_dst, position, 1), row_max, row_total)
        return lax.dot_general(shares.astype(jnp.bfloat16), grad_twice, (((0,), (0,)), ((), ())), preferred_element_type=jnp.float32)
    adjoint_sum = lax.map(back_block, blocks).reshape(SENSORS, -1)
    carried = (grad_once.astype(jnp.float32) + adjoint_sum).astype(jnp.bfloat16)
    row_delta = lax.optimization_barrier(jnp.sum(grad_twice.astype(jnp.float32) * second_full + carried.astype(jnp.float32) * diffused_full, axis=1))

    def score_grad(src_part, row_top, row_sum, twice_part, carried_part, delta_part, dst_part, diff_part, hidden_part):
        scores, shares = tile_probs(src_part, dst_part, row_top, row_sum)
        dweights = pair_dot(twice_part, diff_part) + pair_dot(carried_part, hidden_part) - delta_part[:, None]
        return jnp.where(scores > 0.0, shares * dweights, 0.0)

    def src_block(position):
        dscore = score_grad(rows_of(emb_src, position, 1), rows_of(row_max, position, 0), rows_of(row_total, position, 0), rows_of(grad_twice, position, 0), rows_of(carried, position, 0), rows_of(row_delta, position, 0), emb_dst, diffused, hidden)
        return jnp.einsum('ej,ij->ei', emb_dst, dscore, precision=highest)

    def dst_block(position):
        dscore = score_grad(emb_src, row_max, row_total, grad_twice, carried, row_delta, rows_of(emb_dst, position, 1), rows_of(diffused, position, 0), rows_of(hidden, position, 0))
        return jnp.einsum('ei,ij->ej', emb_src, dscore, precision=highest)
    grad_src = jnp.transpose(lax.map(src_block, blocks), (1, 0, 2)).reshape(EMB, -1)
    grad_dst = jnp.transpose(lax.map(dst_block, blocks), (1, 0, 2)).reshape(EMB, -1)
    return (layer_out, grad_src, grad_dst, grad_mix)
```

```python
import math

import jax
import jax.numpy as jnp
from jax import lax
from jax.experimental import pallas as pl
from jax.experimental.pallas import tpu as pltpu
from jax.sharding import PartitionSpec as P

STEPS = 12


highest = lax.Precision.HIGHEST


def front(readings, start_proj, conv_weight):
    sensors_here = readings.shape[0]
    channels = start_proj.shape[1]
    padded = jnp.concatenate(
        [jnp.zeros(readings.shape[:-1] + (1,), jnp.float32), readings], axis=-1
    )
    inputs = (padded[..., None] * start_proj[0] + start_proj[1]).astype(jnp.bfloat16)
    paired = jnp.concatenate([inputs[:, :, :-1, :], inputs[:, :, 1:, :]], axis=-1).reshape(
        -1, 2 * channels
    )
    gate_terms = jnp.dot(paired, conv_weight, preferred_element_type=jnp.float32)
    hidden = (jnp.tanh(gate_terms[:, :channels]) * jax.nn.sigmoid(gate_terms[:, channels:])).astype(
        jnp.bfloat16
    )
    return (hidden.reshape(sensors_here, -1), inputs[:, :, 1:, :].reshape(sensors_here, -1))


def mixing(residual, hidden, diffused, second, mix_weight):
    channels = mix_weight.shape[1]
    stacked = jnp.concatenate(
        [member.reshape(-1, channels) for member in (hidden, diffused, second)], axis=1
    )
    summed = residual.reshape(-1, channels).astype(jnp.float32) + jnp.dot(
        stacked, mix_weight, preferred_element_type=jnp.float32
    )
    return (summed.astype(jnp.bfloat16).reshape(hidden.shape[0], -1), stacked)


def channel_grads(out_grad, mix_weight):
    channels = mix_weight.shape[1]
    row_count = out_grad.shape[0]
    flat_grad = out_grad.reshape(-1, channels)
    dims = (((1,), (1,)), ((), ()))
    grad_once = lax.dot_general(
        flat_grad, mix_weight[channels : 2 * channels], dims, preferred_element_type=jnp.float32
    )
    grad_twice = lax.dot_general(
        flat_grad, mix_weight[2 * channels :], dims, preferred_element_type=jnp.float32
    )
    return (
        grad_once.astype(jnp.bfloat16).reshape(row_count, -1),
        grad_twice.astype(jnp.bfloat16).reshape(row_count, -1),
    )


def tile_probs(rows_emb, cols_emb, row_max, row_total):
    scores = jnp.einsum("ei,ej->ij", rows_emb, cols_emb, precision=highest)
    shares = jnp.exp(jnp.maximum(scores, 0.0) - row_max[:, None]) / row_total[:, None]
    return (scores, shares)


def pair_dot(left, right):
    return lax.dot_general(
        left, right, (((1,), (1,)), ((), ())), preferred_element_type=jnp.float32
    )


def in_blocks(step_fn, status, members, axis_dim):
    amount = members[0].shape[axis_dim]
    span_size = math.gcd(amount, 512)

    def advance(position, current):
        opening = position * span_size
        sliced = tuple(
            (lax.dynamic_slice_in_dim(member, opening, span_size, axis_dim) for member in members)
        )
        return step_fn(current, sliced, opening)

    return lax.fori_loop(0, amount // span_size, advance, status)


def score_grads(status, emb_src, cols_dst, offset, scores, shares, dweights):
    grad_rows, grad_cols = status
    dscore = jnp.where(scores > 0.0, shares * dweights, 0.0)
    grad_rows = grad_rows + jnp.einsum("ej,ij->ei", cols_dst, dscore, precision=highest)
    span_size = dscore.shape[1]
    current = lax.dynamic_slice_in_dim(grad_cols, offset, span_size, 1)
    added = current + jnp.einsum("ei,ij->ej", emb_src, dscore, precision=highest)
    return (grad_rows, lax.dynamic_update_slice_in_dim(grad_cols, added, offset, 1))


def per_device(
    series, starts, sensor_order, emb_src, emb_dst, start_proj, conv_weight, mix_weight, out_grad
):
    local_rows = sensor_order.shape[0]
    embed_dim = emb_src.shape[0]
    channels = start_proj.shape[1]
    all_rows = local_rows * lax.axis_size("sensor")
    windows = jax.vmap(lambda first_step: lax.dynamic_slice_in_dim(series, first_step, STEPS, 0))(
        starts
    )
    flat_windows = windows.reshape(-1, local_rows)
    window_rows = flat_windows.shape[0]

    def pick_step(status, members, offset):
        readings_sum, dst_all = status
        block_windows, block_dst = members
        span_size = block_windows.shape[1]
        onehot = (sensor_order[:, None] == offset + lax.iota(jnp.int32, span_size)[None, :]).astype(
            jnp.float32
        )
        readings_sum = readings_sum + jnp.einsum(
            "wj,pj->wp", block_windows, onehot, precision=highest
        )
        return (readings_sum, lax.dynamic_update_slice_in_dim(dst_all, block_dst, offset, 1))

    readings_sum, dst_all = in_blocks(
        pick_step,
        (
            jnp.zeros((window_rows, local_rows), jnp.float32),
            jnp.zeros((embed_dim, all_rows), jnp.float32),
        ),
        (
            lax.all_gather(flat_windows, "sensor", axis=1, tiled=True),
            lax.all_gather(emb_dst, "sensor", axis=1, tiled=True),
        ),
        1,
    )
    readings = readings_sum.T.reshape(local_rows, -1, STEPS)
    hidden, residual = front(readings, start_proj, conv_weight)
    feat_cols = hidden.shape[1]
    span_all = math.gcd(all_rows, 512)

    def stat_step(position, current):
        best_score, summed = current
        cols_dst = lax.dynamic_slice_in_dim(dst_all, position * span_all, span_all, 1)
        scores = jnp.maximum(jnp.einsum("ei,ej->ij", emb_src, cols_dst, precision=highest), 0.0)
        new_best = jnp.maximum(best_score, jnp.max(scores, axis=1))
        summed = summed * jnp.exp(best_score - new_best) + jnp.sum(
            jnp.exp(scores - new_best[:, None]), axis=1
        )
        return (new_best, summed)

    row_max, row_total = lax.fori_loop(
        0,
        all_rows // span_all,
        stat_step,
        (jnp.zeros((local_rows,), jnp.float32), jnp.zeros((local_rows,), jnp.float32)),
    )
    grad_once, grad_twice = channel_grads(out_grad, mix_weight)

    def spread_step(status, members, offset):
        block_feat = members[0]
        cols_dst = lax.dynamic_slice_in_dim(dst_all, offset, block_feat.shape[0], 1)
        scores, shares = tile_probs(emb_src, cols_dst, row_max, row_total)
        return status + jnp.dot(
            shares.astype(jnp.bfloat16), block_feat, preferred_element_type=jnp.float32
        )

    first_init = jnp.zeros((local_rows, feat_cols), jnp.float32)
    first_result = in_blocks(
        spread_step, first_init, (lax.all_gather(hidden, "sensor", axis=0, tiled=True),), 0
    )
    diffused = first_result.astype(jnp.bfloat16)

    def plain_step(status, members, offset):
        accumulated, grad_rows, grad_cols = status
        return (spread_step(accumulated, members, offset), grad_rows, grad_cols)

    second_init = (
        jnp.zeros((local_rows, feat_cols), jnp.float32),
        jnp.zeros((embed_dim, local_rows), jnp.float32),
        jnp.zeros((embed_dim, all_rows), jnp.float32),
    )
    second_result = in_blocks(
        plain_step, second_init, (lax.all_gather(diffused, "sensor", axis=0, tiled=True),), 0
    )
    second_full, grad_rows, grad_cols = second_result
    second = second_full.astype(jnp.bfloat16)
    layer_out, stacked = mixing(residual, hidden, diffused, second, mix_weight)
    mix_part = lax.dot_general(
        stacked,
        out_grad.reshape(-1, channels),
        (((0,), (0,)), ((), ())),
        preferred_element_type=jnp.float32,
    )
    span_size = math.gcd(lax.axis_size("sensor") * local_rows, 512)

    def piece_term(position):
        cols_dst = lax.dynamic_slice_in_dim(dst_all, position * span_size, span_size, 1)
        scores, shares = tile_probs(emb_src, cols_dst, row_max, row_total)
        return lax.dot_general(
            shares.astype(jnp.bfloat16),
            grad_twice,
            (((0,), (0,)), ((), ())),
            preferred_element_type=jnp.float32,
        )

    adjoint_sum = lax.psum_scatter(
        lax.map(
            piece_term,
            jnp.arange(lax.axis_size("sensor") * local_rows // span_size, dtype=jnp.int32),
        ).reshape(lax.axis_size("sensor") * local_rows, -1),
        "sensor",
        scatter_dimension=0,
        tiled=True,
    )
    carried = (grad_once.astype(jnp.float32) + adjoint_sum).astype(jnp.bfloat16)
    row_delta = jnp.sum(
        grad_twice.astype(jnp.float32) * second_full + carried.astype(jnp.float32) * first_result,
        axis=1,
    )

    def pair_step(status, members, offset):
        block_hidden, block_diff = members
        cols_dst = lax.dynamic_slice_in_dim(dst_all, offset, block_hidden.shape[0], 1)
        scores, shares = tile_probs(emb_src, cols_dst, row_max, row_total)
        dweights = (
            pair_dot(grad_twice, block_diff) + pair_dot(carried, block_hidden) - row_delta[:, None]
        )
        return score_grads(status, emb_src, cols_dst, offset, scores, shares, dweights)

    grad_rows, grad_cols = in_blocks(
        pair_step,
        (grad_rows, grad_cols),
        (
            lax.all_gather(hidden, "sensor", axis=0, tiled=True),
            lax.all_gather(diffused, "sensor", axis=0, tiled=True),
        ),
        0,
    )
    grad_dst = lax.psum_scatter(grad_cols, "sensor", scatter_dimension=1, tiled=True)
    grad_mix = lax.psum(mix_part, "sensor")
    return (layer_out, grad_rows, grad_dst, grad_mix)


NT = (((1,), (1,)), ((), ()))
TN = (((0,), (0,)), ((), ()))
f32 = jnp.float32
bf16 = jnp.bfloat16
SLOT = 48
WIDE = 256
LOG2_E = math.log2(math.e)
NEAR = 3


def iota(shape, dim):
    return lax.broadcasted_iota(jnp.int32, shape, dim)


def ones_where(mask):
    return jnp.where(mask, 1.0, 0.0).astype(bf16)


def nn(left, right):
    return jnp.dot(left, right, preferred_element_type=f32)


def nt(left, right):
    return lax.dot_general(left, right, NT, preferred_element_type=f32)


def tn(left, right):
    return lax.dot_general(left, right, TN, preferred_element_type=f32)


def halves(value):
    high = value.astype(bf16)
    return high, (value - high.astype(f32)).astype(bf16)


def thirds(value):
    high, middle = halves(value)
    return high, middle, (value - high.astype(f32) - middle.astype(f32)).astype(bf16)


def gather_kernel(
    n, starts, series_in, order_in, src_in, dst_in, proj_in, conv_in, mix_in, out_grad_in,
    diffused, back, twice, left, right, stats,
    layer_out, shares_src, masked_src, shares_dst, dots_src, dots_dst, mixed_grad,
    series, order, src, dst, start_proj, conv, mix, small, given, inputs, picked, weights, mixed_one, partial,
    hidden, mixed_two, grads, ahead, mix_big,
    load_sem, small_send, small_recv, big_send, big_recv,
):
    me = lax.axis_index("sensor")
    total = SLOT * n
    loads = [
        pltpu.make_async_copy(source, target, load_sem.at[at])
        for at, (source, target) in enumerate(
            [
                (series_in, series), (order_in, order),
                (src_in, src), (dst_in, dst),
                (out_grad_in, given.at[0, 0]), (conv_in, conv), (mix_in, mix), (proj_in, start_proj),
            ]
        )
    ]
    barrier = pltpu.get_barrier_semaphore()
    for k in range(1, n):
        pl.semaphore_signal(
            barrier, inc=1, device_id={"sensor": lax.rem(me + k, n)},
            device_id_type=pl.DeviceIdType.MESH,
        )
    for load in loads:
        load.start()

    wanted = ones_where(iota((16, series.shape[1]), 1) == iota((16, series.shape[1]), 0) + starts[0])
    for load in loads[:4]:
        load.wait()
    window = sum(nt(wanted, part) for part in thirds(series[...]))
    numbers = order[...].astype(f32)
    numbers = jnp.concatenate(
        [numbers[:, 0:16], numbers[:, 16:32], numbers[:, 32:48], jnp.zeros((13, 16), f32)], axis=0
    )
    small[0, 0] = jnp.concatenate(
        [
            jnp.concatenate([src[...], window[0:6, :]], axis=0), numbers,
            jnp.concatenate([dst[...], window[6:12, :]], axis=0), jnp.zeros((16, 16), f32),
        ],
        axis=1,
    )
    loads[4].wait()
    pl.semaphore_wait(barrier, n - 1)

    def remote(source, target, send, recv, peer):
        return pltpu.make_async_remote_copy(
            src_ref=source, dst_ref=target, send_sem=send, recv_sem=recv,
            device_id={"sensor": peer}, device_id_type=pl.DeviceIdType.MESH,
        )

    odd = lax.rem(me, 2)
    sibling = me + 1 - 2 * odd
    half = n // 2

    def spread_own(ref, send, recv):
        copies = []
        for k in list(range(1, half)) + [0]:
            if k == 0:
                target, peer = ref.at[lax.rem(odd + half - 1, half), 1], sibling
            else:
                target, peer = ref.at[half - k, 0], lax.rem(me + 2 * k, n)
            copy = remote(
                ref.at[0, 0], target, send.at[min(k, 1)], recv.at[k], peer
            )
            copy.start()
            copies.append(copy)
        return copies

    def others(ref, first, parity):
        return ref.at[pl.ds(first, half - 1), parity]

    def arrived(ref, send, recv):
        return remote(others(ref, 1, 0), others(ref, 1, 0), send.at[1], recv.at[1], sibling)

    def small_piece(k):
        part = small.at[half - k, 0]
        return remote(part, part, small_send.at[1], small_recv.at[k], sibling)

    plane, last = me // 4, n // 4 - 1
    keys = [lax.rem(me - (n - 4 + odd + 2 * j) + n, n) // 2 for j in (0, 1)]

    def wait_last_plane():
        for key in keys:
            @pl.when(key > 0)
            def _(key=key):
                small_piece(key).wait_recv()

    def wait_other_planes():
        for k in range(1, half):
            @pl.when((keys[0] != k) & (keys[1] != k))
            def _(k=k):
                small_piece(k).wait_recv()

    def pass_on(ref, send, recv):
        copy = remote(others(ref, 1, 0), others(ref, odd, 1), send.at[2], recv.at[half], sibling)
        copy.start()
        return copy

    def wait_rest(copies, passed):
        copies[-1].wait_recv()
        passed.wait_recv()

    def wait_sent(ref, send, recv, copies, passed):
        arrived(ref, send, recv).wait_send()
        copies[-1].wait_send()
        passed.wait_send()

    small_copies = spread_own(small, small_send, small_recv)
    def big_copy(k):
        group = 0 if k == 0 else 1 + (k >= NEAR)
        if k == 0:
            target, peer = given.at[lax.rem(odd + half - 1, half), 1], sibling
        else:
            target, peer = given.at[half - k, 0], lax.rem(me + 2 * k, n)
        return remote(given.at[0, 0], target, big_send.at[group], big_recv.at[group], peer)

    def waits(k):
        facing = (k == half - 1) & (lax.rem(me // 2, 2) == 1)
        return (plane > 0) & (me // 2 + k >= n // 2) & jnp.logical_not(facing)

    def send_big(late):
        for k in range(1, half):
            @pl.when(waits(k) if late else jnp.logical_not(waits(k)))
            def _(k=k):
                big_copy(k).start()

    send_big(False)
    big_copies = [big_copy(0)]
    big_copies[0].start()
    groups = {1: (half - NEAR + 1, NEAR - 1), 2: (1, half - NEAR)}

    def big_arrived(group):
        part = given.at[pl.ds(*groups[group]), 0]
        return remote(part, part, big_send.at[group], big_recv.at[group], sibling)

    big_passed = []

    def pass_big(group):
        first, count = groups[group]
        big_arrived(group).wait_recv()
        copy = remote(
            given.at[pl.ds(first, count), 0], given.at[pl.ds(first - 1 + odd, count), 1],
            big_send.at[2 + group], big_recv.at[2 + group], sibling,
        )
        copy.start()
        big_passed.append(copy)


    for load in loads[5:]:
        load.wait()

    spread = ones_where(
        iota((256, 64), 1) == (iota((256, 64), 0) >> 7) * 32 + (iota((256, 64), 0) & 31)
    )
    taps = nt(spread, conv[...]).astype(bf16)
    shape = (256, 160)
    lead = (iota(shape, 1) >> 5) - ((iota(shape, 0) & 127) >> 5)
    pick = iota((64, 160), 0) == (iota((64, 160), 1) & 31)
    later = iota((64, 160), 0) == (iota((64, 160), 1) & 31) + 32
    band = jnp.where(lead == 0, nn(taps, ones_where(pick)), 0.0)
    band = jnp.where(lead == 1, nn(taps, ones_where(later)), band)
    band = jnp.where(iota(shape, 0) < 128, band, 0.5 * band).astype(bf16)
    shape = (384, 32)
    spread = ones_where(iota(shape, 1) == (iota(shape, 0) & 31))
    rows = nn(spread, mix[...])
    rows = jnp.where((iota((384, 96), 1) >> 5) == (iota((384, 96), 0) >> 7), rows, 0.0).astype(bf16)
    spread = ones_where((iota((96, 128), 0) & 31) == (iota((96, 128), 1) & 31))
    shape = (384, 128)
    mix_big[...] = jnp.where(
        ((iota(shape, 0) & 127) >> 5) == (iota(shape, 1) >> 5), nn(rows, spread), 0.0
    ).astype(bf16)
    columns = jnp.concatenate(
        [jnp.concatenate([start_proj[...]] * 4, axis=1), jnp.zeros((126, 128), f32)], axis=0
    ).T
    weight, bias = columns[0:32, 0:1], columns[0:32, 1:2]
    inputs[0:32, :] = jnp.broadcast_to(bias, (32, total)).astype(bf16)

    wait_last_plane()

    send_big(True)
    wait_other_planes()
    small_passed = pass_on(small, small_send, small_recv)

    wait_rest(small_copies, small_passed)

    by_lane = list(range(0, n, 2)) + list(range(1, n, 2))

    def across(lanes):
        whole = jnp.concatenate([small[k // 2, k % 2, :, lanes] for k in by_lane], axis=1)
        return jnp.where(iota((16, total), 0) < 10, whole, 0.0)

    high, middle, low = thirds(across(slice(0, SLOT)) * LOG2_E)
    left[...] = jnp.concatenate([high, middle, low, high, high, middle], axis=0)
    high, middle, low = thirds(across(slice(64, 64 + SLOT)))
    right[...] = jnp.concatenate([high, middle, high, low, middle, high], axis=0)

    numbers = jnp.concatenate([small[:, :, q, 48:64].reshape(n, 16) for q in range(3)], axis=1)
    numbers = jnp.concatenate([numbers[k : k + 1, :] for k in by_lane], axis=1).astype(jnp.int32)
    owner = (numbers * 1366) >> 16
    place = numbers - SLOT * owner
    owner = (owner - me + n) & (n - 1)
    high, low = halves(small[:, :, 8:16, :].reshape(8 * n, 128))
    found = jnp.concatenate([high, low], axis=1)

    def pick_steps(offset):
        onehot = ones_where(iota((128, total), 0) == place + offset)
        steps = nn(found, jnp.concatenate([onehot, onehot], axis=0))
        terms = [jnp.where(owner == k, steps[8 * k : 8 * k + 8, :], 0.0) for k in range(n)]
        while len(terms) > 1:
            terms = [a + b for a, b in zip(terms[::2], terms[1::2])]
        return terms[0]

    picked[0:8, :] = pick_steps(0)
    picked[8:16, :] = pick_steps(64)
    for t in range(STEPS):
        inputs[32 * t + 32 : 32 * t + 64, :] = (picked[t + 2 + 2 * (t // 6) : t + 3 + 2 * (t // 6), :] * weight + bias).astype(bf16)
    for b in range(3):
        terms = nn(band, inputs[128 * b : 128 * b + 160, :])
        gated = jnp.tanh(terms[:128, :]) * (0.5 * jnp.tanh(terms[128:, :]) + 0.5)
        hidden[128 * b : 128 * b + 128, :] = gated.astype(bf16)

    chunks = [slice(at, at + WIDE) for at in range(0, total, WIDE)]
    tiles = [slice(128 * b, 128 * b + 128) for b in range(3)]
    for cols in chunks:
        scores = tn(right[...], left[:, cols])
        top = jnp.maximum(jnp.max(scores, axis=0, keepdims=True), 0.0)
        terms = jnp.exp2(jnp.maximum(scores, 0.0) - top)
        weights[:, cols] = terms.astype(bf16)
        inverse = 1.0 / jnp.sum(terms, axis=0, keepdims=True)
        stats[0:1, cols] = top
        stats[1:2, cols] = inverse
    for cols in chunks:
        result = nn(hidden[...], weights[:, cols]) * stats[1:2, cols]
        diffused[:, cols] = result.astype(bf16)
    for rows in tiles:
        both = nn(mix_big[128:384, :], diffused[rows, :])
        mixed_one[rows, :] = both[:128, :]
        mixed_two[rows, :] = both[128:, :].astype(bf16)
        more = nn(mix_big[128:384, :], hidden[rows, :])
        ahead[rows, :] = (both[128:, :] + more[:128, :]).astype(bf16)
        twice[rows, :] = more[128:, :].astype(bf16)

    pass_big(1)
    for cols in chunks:
        result = nn(mixed_two[...], weights[:, cols]) * stats[1:2, cols]
        mixed_one[:, cols] = mixed_one[:, cols] + result

    own = slice(0, 128)
    for rows in tiles:
        summed = inputs[32 + rows.start : 160 + rows.start, own].astype(f32)
        summed = summed + nn(mix_big[0:128, :], hidden[rows, own]) + mixed_one[rows, own]
        layer_out[:, rows] = summed.T[0:SLOT, :].astype(bf16)
    scores = tn(right[:, own], left[...])[0:SLOT, :]
    shares = jnp.exp2(jnp.maximum(scores, 0.0) - stats[0:1, :]) * stats[1:2, :]
    shares_dst[...] = jnp.where(scores > 0.0, shares, 0.0)
    scores = tn(left[:, own], right[...])[0:SLOT, :]
    top = jnp.maximum(jnp.max(scores, axis=1, keepdims=True), 0.0)
    terms = jnp.exp2(jnp.maximum(scores, 0.0) - top)
    shares = terms * (1.0 / jnp.sum(terms, axis=1, keepdims=True))
    shares_src[...] = shares
    masked_src[...] = jnp.where(scores > 0.0, shares, 0.0)
    dots_src[...] = nn(given[0, 0], ahead[...])

    pass_big(2)

    def take(parity):
        cols = slice(SLOT * half * parity, SLOT * half * (parity + 1))
        part = given[:, parity].reshape(SLOT * half, 384).T
        grads[:, cols] = part
        part = part.astype(f32)
        stats[2:3, cols] = jnp.sum(part * mixed_one[:, cols], axis=0, keepdims=True)
        inputs[0:384, cols] = (part * stats[1:2, cols]).astype(bf16)

    def use(parity):
        cols = slice(SLOT * half * parity, SLOT * half * (parity + 1))
        dots_dst[:, cols] = tn(ahead[:, own], grads[:, cols])[0:SLOT, :]
        natural = given[:, parity].reshape(SLOT * half, 384)
        return sum(
            nn(jnp.concatenate([hidden[rows, cols], diffused[rows, cols]], axis=0), natural[:, rows])
            for rows in tiles
        )

    take(0)
    mixed_grad[...] = use(0)
    early = slice(0, SLOT * half)
    for cols in chunks:
        partial[:, cols] = nt(inputs[0:384, early], weights[cols, early])
    for copy in big_copies[-1:] + big_passed:
        copy.wait_recv()
    take(1)
    for cols in chunks:
        result = partial[:, cols] + nt(inputs[0:384, SLOT * half : total], weights[cols, SLOT * half : total])
        back[:, cols] = result.astype(bf16)
        stats[2:3, cols] = stats[2:3, cols] + jnp.sum(
            result * mixed_two[:, cols].astype(f32), axis=0, keepdims=True
        )

    mixed_grad[...] = mixed_grad[...] + use(1)
    wait_sent(small, small_send, small_recv, small_copies, small_passed)
    big_arrived(1).wait_send()
    big_arrived(2).wait_send()
    for copy in big_copies[-1:] + big_passed:
        copy.wait_send()


def finish_kernel(
    n, diffused, back, twice, left, right, stats, layer_out, shares_src, masked_src, shares_dst, dots_src, dots_dst, mixed_grad,
    layer_out_to, grad_src_to, grad_dst_to, grad_mix_to,
    grad_src, grad_dst, grad_mix, store_sem,
):
    stores = [
        pltpu.make_async_copy(source, target, store_sem.at[at])
        for at, (source, target) in enumerate(
            [
                (layer_out, layer_out_to), (grad_mix, grad_mix_to),
                (grad_src, grad_src_to), (grad_dst, grad_dst_to),
            ]
        )
    ]
    stores[0].start()
    tiles = [slice(128 * b, 128 * b + 128) for b in range(3)]
    own = slice(0, 128)

    def score_grad(value, stacked):
        high, low = halves(value)
        return nt(stacked, jnp.concatenate([high, low], axis=0))

    dots_to = dots_dst[...] + tn(twice[:, own], back[...])[0:SLOT, :] - stats[2:3, :]
    dots_from = dots_src[...] + tn(back[:, own], twice[...])[0:SLOT, :]
    delta = jnp.sum(shares_src[...] * dots_from, axis=1, keepdims=True)
    to = score_grad(shares_dst[...] * dots_to, left[0:48, :])
    source = score_grad(masked_src[...] * (dots_from - delta), right[0:64, :])
    again = sum(nt(diffused[rows, :], back[rows, :]) for rows in tiles)
    to = to[0:16, :] + to[16:32, :] + to[32:48, :]
    source = source[0:16, :] + source[16:32, :] + source[48:64, :]
    grad_dst[...] = (to[0:10, 0:SLOT] + to[0:10, SLOT : 2 * SLOT]) * (1.0 / LOG2_E)
    grad_src[...] = source[0:10, 0:SLOT] + source[0:10, SLOT : 2 * SLOT]
    mixed = [
        sum(block[32 * t : 32 * (t + 1), 32 * t : 32 * (t + 1)] for t in range(4))
        for block in (mixed_grad[0:128, :], mixed_grad[128:256, :], again)
    ]
    mixed = jnp.concatenate(mixed + [jnp.zeros((32, 32), f32)], axis=0)
    mixed = jnp.concatenate([mixed, jnp.zeros((128, 96), f32)], axis=1)
    grad_mix[...] = mixed.T[0:32, 0:96]
    for store in stores[1:]:
        store.start()
    for store in stores:
        store.wait()


def whole_in_kernel(
    series, starts, sensor_order, emb_src, emb_dst, start_proj, conv_weight, mix_weight, out_grad
):
    n = lax.axis_size("sensor")
    total = SLOT * n
    vmem = pl.BlockSpec(memory_space=pltpu.VMEM)
    anywhere = pl.BlockSpec(memory_space=pltpu.HBM)
    dma = pltpu.SemaphoreType.DMA
    wide = jax.ShapeDtypeStruct((384, total), bf16)
    strip = jax.ShapeDtypeStruct((SLOT, total), f32)
    stacked = jax.ShapeDtypeStruct((96, total), bf16)
    operands = (
        series.T, sensor_order.reshape(1, -1), emb_src, emb_dst, start_proj, conv_weight,
        mix_weight.T, out_grad,
    )
    operands = tuple(pltpu.with_memory_space_constraint(operand, pltpu.HBM) for operand in operands)
    staged = [operands[at] for at in (0, 1, 2, 3, 4, 5, 6)]
    held = pl.pallas_call(
        lambda *refs: gather_kernel(n, *refs),
        out_shape=(
            wide, wide, wide, stacked, stacked,
            jax.ShapeDtypeStruct((8, total), f32),
            jax.ShapeDtypeStruct((SLOT, 384), bf16),
            strip, strip, strip, strip, strip,
            jax.ShapeDtypeStruct((256, 128), f32),
        ),
        in_specs=[pl.BlockSpec(memory_space=pltpu.SMEM)] + [anywhere] * 8,
        out_specs=(vmem,) * 13,
        scratch_shapes=[pltpu.VMEM(operand.shape, operand.dtype) for operand in staged]
        + [
            pltpu.VMEM((n // 2, 2, 16, 128), f32),
            pltpu.VMEM((n // 2, 2, SLOT, 384), bf16),
            pltpu.VMEM((416, total), bf16),
            pltpu.VMEM((16, total), f32),
            pltpu.VMEM((total, total), bf16),
            pltpu.VMEM((384, total), f32),
            pltpu.VMEM((384, total), f32),
            pltpu.VMEM((384, total), bf16),
            pltpu.VMEM((384, total), bf16),
            pltpu.VMEM((384, total), bf16),
            pltpu.VMEM((384, total), bf16),
            pltpu.VMEM((384, 128), bf16),
            dma((8,)),
            dma((3,)),
            dma((n // 2 + 1,)),
            dma((5,)),
            dma((5,)),
        ],
        compiler_params=pltpu.CompilerParams(
            collective_id=0, has_side_effects=True, vmem_limit_bytes=32 * 2**20
        ),
    )(starts, *operands)
    outs = (
        jax.ShapeDtypeStruct((48, 384), bf16),
        jax.ShapeDtypeStruct((10, 48), f32),
        jax.ShapeDtypeStruct((10, 48), f32),
        jax.ShapeDtypeStruct((32, 96), f32),
    )
    layer_out, grad_src, grad_dst, grad_mix = pl.pallas_call(
        lambda *refs: finish_kernel(n, *refs),
        out_shape=outs,
        in_specs=[vmem] * 13,
        out_specs=(anywhere,) * 4,
        scratch_shapes=[pltpu.VMEM(out.shape, out.dtype) for out in outs[1:]] + [dma((4,))],
        compiler_params=pltpu.CompilerParams(vmem_limit_bytes=32 * 2**20),
    )(*held)
    return layer_out, grad_src, grad_dst, grad_mix.T


def layer_on_device(*operands):
    if lax.axis_size("sensor") == 16 and operands[2].shape[0] == 48:
        return whole_in_kernel(*operands)
    return per_device(*operands)


def solution(mesh):
    placed = (
        P(None, ("groups", "sensor")),
        P("groups"),
        P(("groups", "sensor")),
        P(None, ("groups", "sensor")),
        P(None, ("groups", "sensor")),
        P(),
        P(),
        P(),
        P(("groups", "sensor"), None),
    )
    return jax.shard_map(
        layer_on_device,
        mesh=mesh,
        in_specs=placed,
        out_specs=(
            P(("groups", "sensor"), None),
            P(None, ("groups", "sensor")),
            P(None, ("groups", "sensor")),
            P("groups", None),
        ),
        check_vma=False,
    )
```

```python
import math

import jax
import jax.numpy as jnp
from jax import lax
from jax.experimental import pallas as pl
from jax.experimental.pallas import tpu as pltpu
from jax.sharding import PartitionSpec as P

STEPS = 12


highest = lax.Precision.HIGHEST


def front(readings, start_proj, conv_weight):
    sensors_here = readings.shape[0]
    channels = start_proj.shape[1]
    padded = jnp.concatenate(
        [jnp.zeros(readings.shape[:-1] + (1,), jnp.float32), readings], axis=-1
    )
    inputs = (padded[..., None] * start_proj[0] + start_proj[1]).astype(jnp.bfloat16)
    paired = jnp.concatenate([inputs[:, :, :-1, :], inputs[:, :, 1:, :]], axis=-1).reshape(
        -1, 2 * channels
    )
    gate_terms = jnp.dot(paired, conv_weight, preferred_element_type=jnp.float32)
    hidden = (jnp.tanh(gate_terms[:, :channels]) * jax.nn.sigmoid(gate_terms[:, channels:])).astype(
        jnp.bfloat16
    )
    return (hidden.reshape(sensors_here, -1), inputs[:, :, 1:, :].reshape(sensors_here, -1))


def mixing(residual, hidden, diffused, second, mix_weight):
    channels = mix_weight.shape[1]
    stacked = jnp.concatenate(
        [member.reshape(-1, channels) for member in (hidden, diffused, second)], axis=1
    )
    summed = residual.reshape(-1, channels).astype(jnp.float32) + jnp.dot(
        stacked, mix_weight, preferred_element_type=jnp.float32
    )
    return (summed.astype(jnp.bfloat16).reshape(hidden.shape[0], -1), stacked)


def channel_grads(out_grad, mix_weight):
    channels = mix_weight.shape[1]
    row_count = out_grad.shape[0]
    flat_grad = out_grad.reshape(-1, channels)
    dims = (((1,), (1,)), ((), ()))
    grad_once = lax.dot_general(
        flat_grad, mix_weight[channels : 2 * channels], dims, preferred_element_type=jnp.float32
    )
    grad_twice = lax.dot_general(
        flat_grad, mix_weight[2 * channels :], dims, preferred_element_type=jnp.float32
    )
    return (
        grad_once.astype(jnp.bfloat16).reshape(row_count, -1),
        grad_twice.astype(jnp.bfloat16).reshape(row_count, -1),
    )


def tile_probs(rows_emb, cols_emb, row_max, row_total):
    scores = jnp.einsum("ei,ej->ij", rows_emb, cols_emb, precision=highest)
    shares = jnp.exp(jnp.maximum(scores, 0.0) - row_max[:, None]) / row_total[:, None]
    return (scores, shares)


def pair_dot(left, right):
    return lax.dot_general(
        left, right, (((1,), (1,)), ((), ())), preferred_element_type=jnp.float32
    )


def in_blocks(step_fn, status, members, axis_dim):
    amount = members[0].shape[axis_dim]
    span_size = math.gcd(amount, 512)

    def advance(position, current):
        opening = position * span_size
        sliced = tuple(
            (lax.dynamic_slice_in_dim(member, opening, span_size, axis_dim) for member in members)
        )
        return step_fn(current, sliced, opening)

    return lax.fori_loop(0, amount // span_size, advance, status)


def score_grads(status, emb_src, cols_dst, offset, scores, shares, dweights):
    grad_rows, grad_cols = status
    dscore = jnp.where(scores > 0.0, shares * dweights, 0.0)
    grad_rows = grad_rows + jnp.einsum("ej,ij->ei", cols_dst, dscore, precision=highest)
    span_size = dscore.shape[1]
    current = lax.dynamic_slice_in_dim(grad_cols, offset, span_size, 1)
    added = current + jnp.einsum("ei,ij->ej", emb_src, dscore, precision=highest)
    return (grad_rows, lax.dynamic_update_slice_in_dim(grad_cols, added, offset, 1))


def per_device(
    series, starts, sensor_order, emb_src, emb_dst, start_proj, conv_weight, mix_weight, out_grad
):
    local_rows = sensor_order.shape[0]
    embed_dim = emb_src.shape[0]
    channels = start_proj.shape[1]
    all_rows = local_rows * lax.axis_size("sensor")
    windows = jax.vmap(lambda first_step: lax.dynamic_slice_in_dim(series, first_step, STEPS, 0))(
        starts
    )
    flat_windows = windows.reshape(-1, local_rows)
    window_rows = flat_windows.shape[0]

    def pick_step(status, members, offset):
        readings_sum, dst_all = status
        block_windows, block_dst = members
        span_size = block_windows.shape[1]
        onehot = (sensor_order[:, None] == offset + lax.iota(jnp.int32, span_size)[None, :]).astype(
            jnp.float32
        )
        readings_sum = readings_sum + jnp.einsum(
            "wj,pj->wp", block_windows, onehot, precision=highest
        )
        return (readings_sum, lax.dynamic_update_slice_in_dim(dst_all, block_dst, offset, 1))

    readings_sum, dst_all = in_blocks(
        pick_step,
        (
            jnp.zeros((window_rows, local_rows), jnp.float32),
            jnp.zeros((embed_dim, all_rows), jnp.float32),
        ),
        (
            lax.all_gather(flat_windows, "sensor", axis=1, tiled=True),
            lax.all_gather(emb_dst, "sensor", axis=1, tiled=True),
        ),
        1,
    )
    readings = readings_sum.T.reshape(local_rows, -1, STEPS)
    hidden, residual = front(readings, start_proj, conv_weight)
    feat_cols = hidden.shape[1]
    span_all = math.gcd(all_rows, 512)

    def stat_step(position, current):
        best_score, summed = current
        cols_dst = lax.dynamic_slice_in_dim(dst_all, position * span_all, span_all, 1)
        scores = jnp.maximum(jnp.einsum("ei,ej->ij", emb_src, cols_dst, precision=highest), 0.0)
        new_best = jnp.maximum(best_score, jnp.max(scores, axis=1))
        summed = summed * jnp.exp(best_score - new_best) + jnp.sum(
            jnp.exp(scores - new_best[:, None]), axis=1
        )
        return (new_best, summed)

    row_max, row_total = lax.fori_loop(
        0,
        all_rows // span_all,
        stat_step,
        (jnp.zeros((local_rows,), jnp.float32), jnp.zeros((local_rows,), jnp.float32)),
    )
    grad_once, grad_twice = channel_grads(out_grad, mix_weight)

    def spread_step(status, members, offset):
        block_feat = members[0]
        cols_dst = lax.dynamic_slice_in_dim(dst_all, offset, block_feat.shape[0], 1)
        scores, shares = tile_probs(emb_src, cols_dst, row_max, row_total)
        return status + jnp.dot(
            shares.astype(jnp.bfloat16), block_feat, preferred_element_type=jnp.float32
        )

    first_init = jnp.zeros((local_rows, feat_cols), jnp.float32)
    first_result = in_blocks(
        spread_step, first_init, (lax.all_gather(hidden, "sensor", axis=0, tiled=True),), 0
    )
    diffused = first_result.astype(jnp.bfloat16)

    def plain_step(status, members, offset):
        accumulated, grad_rows, grad_cols = status
        return (spread_step(accumulated, members, offset), grad_rows, grad_cols)

    second_init = (
        jnp.zeros((local_rows, feat_cols), jnp.float32),
        jnp.zeros((embed_dim, local_rows), jnp.float32),
        jnp.zeros((embed_dim, all_rows), jnp.float32),
    )
    second_result = in_blocks(
        plain_step, second_init, (lax.all_gather(diffused, "sensor", axis=0, tiled=True),), 0
    )
    second_full, grad_rows, grad_cols = second_result
    second = second_full.astype(jnp.bfloat16)
    layer_out, stacked = mixing(residual, hidden, diffused, second, mix_weight)
    mix_part = lax.dot_general(
        stacked,
        out_grad.reshape(-1, channels),
        (((0,), (0,)), ((), ())),
        preferred_element_type=jnp.float32,
    )
    span_size = math.gcd(lax.axis_size("sensor") * local_rows, 512)

    def piece_term(position):
        cols_dst = lax.dynamic_slice_in_dim(dst_all, position * span_size, span_size, 1)
        scores, shares = tile_probs(emb_src, cols_dst, row_max, row_total)
        return lax.dot_general(
            shares.astype(jnp.bfloat16),
            grad_twice,
            (((0,), (0,)), ((), ())),
            preferred_element_type=jnp.float32,
        )

    adjoint_sum = lax.psum_scatter(
        lax.map(
            piece_term,
            jnp.arange(lax.axis_size("sensor") * local_rows // span_size, dtype=jnp.int32),
        ).reshape(lax.axis_size("sensor") * local_rows, -1),
        "sensor",
        scatter_dimension=0,
        tiled=True,
    )
    carried = (grad_once.astype(jnp.float32) + adjoint_sum).astype(jnp.bfloat16)
    row_delta = jnp.sum(
        grad_twice.astype(jnp.float32) * second_full + carried.astype(jnp.float32) * first_result,
        axis=1,
    )

    def pair_step(status, members, offset):
        block_hidden, block_diff = members
        cols_dst = lax.dynamic_slice_in_dim(dst_all, offset, block_hidden.shape[0], 1)
        scores, shares = tile_probs(emb_src, cols_dst, row_max, row_total)
        dweights = (
            pair_dot(grad_twice, block_diff) + pair_dot(carried, block_hidden) - row_delta[:, None]
        )
        return score_grads(status, emb_src, cols_dst, offset, scores, shares, dweights)

    grad_rows, grad_cols = in_blocks(
        pair_step,
        (grad_rows, grad_cols),
        (
            lax.all_gather(hidden, "sensor", axis=0, tiled=True),
            lax.all_gather(diffused, "sensor", axis=0, tiled=True),
        ),
        0,
    )
    grad_dst = lax.psum_scatter(grad_cols, "sensor", scatter_dimension=1, tiled=True)
    grad_mix = lax.psum(mix_part, "sensor")
    return (layer_out, grad_rows, grad_dst, grad_mix)


NT = (((1,), (1,)), ((), ()))
TN = (((0,), (0,)), ((), ()))
f32 = jnp.float32
bf16 = jnp.bfloat16
SLOT = 48
WIDE = 256
LOG2_E = math.log2(math.e)
NEAR = 3


def iota(shape, dim):
    return lax.broadcasted_iota(jnp.int32, shape, dim)


def ones_where(mask):
    return jnp.where(mask, 1.0, 0.0).astype(bf16)


def nn(left, right):
    return jnp.dot(left, right, preferred_element_type=f32)


def nt(left, right):
    return lax.dot_general(left, right, NT, preferred_element_type=f32)


def tn(left, right):
    return lax.dot_general(left, right, TN, preferred_element_type=f32)


def halves(value):
    high = value.astype(bf16)
    return high, (value - high.astype(f32)).astype(bf16)


def thirds(value):
    high, middle = halves(value)
    return high, middle, (value - high.astype(f32) - middle.astype(f32)).astype(bf16)


def gather_kernel(
    n, starts, series_in, order_in, src_in, dst_in, proj_in, conv_in, mix_in, out_grad_in,
    diffused, back, twice, left, right, stats,
    layer_out, shares_src, masked_src, shares_dst, dots_src, dots_dst, mixed_grad,
    series, order, src, dst, start_proj, conv, mix, small, given, inputs, picked, weights, mixed_one, partial,
    hidden, mixed_two, grads, ahead, mix_big,
    load_sem, small_send, small_recv, big_send, big_recv,
):
    me = lax.axis_index("sensor")
    total = SLOT * n
    loads = [
        pltpu.make_async_copy(source, target, load_sem.at[at])
        for at, (source, target) in enumerate(
            [
                (series_in, series), (order_in, order),
                (src_in, src), (dst_in, dst),
                (out_grad_in, given.at[0, 0]), (conv_in, conv), (mix_in, mix), (proj_in, start_proj),
            ]
        )
    ]
    barrier = pltpu.get_barrier_semaphore()
    for k in range(1, n):
        pl.semaphore_signal(
            barrier, inc=1, device_id={"sensor": lax.rem(me + k, n)},
            device_id_type=pl.DeviceIdType.MESH,
        )
    for load in loads:
        load.start()

    wanted = ones_where(iota((16, series.shape[1]), 1) == iota((16, series.shape[1]), 0) + starts[0])
    for load in loads[:4]:
        load.wait()
    window = sum(nt(wanted, part) for part in halves(series[...]))
    numbers = order[...].astype(f32)
    numbers = jnp.concatenate(
        [numbers[:, 0:16], numbers[:, 16:32], numbers[:, 32:48], jnp.zeros((13, 16), f32)], axis=0
    )
    small[0, 0] = jnp.concatenate(
        [
            jnp.concatenate([src[...], window[0:6, :]], axis=0), numbers,
            jnp.concatenate([dst[...], window[6:12, :]], axis=0), jnp.zeros((16, 16), f32),
        ],
        axis=1,
    )
    loads[4].wait()
    pl.semaphore_wait(barrier, n - 1)

    def remote(source, target, send, recv, peer):
        return pltpu.make_async_remote_copy(
            src_ref=source, dst_ref=target, send_sem=send, recv_sem=recv,
            device_id={"sensor": peer}, device_id_type=pl.DeviceIdType.MESH,
        )

    odd = lax.rem(me, 2)
    sibling = me + 1 - 2 * odd
    half = n // 2

    def spread_own(ref, send, recv):
        copies = []
        for k in list(range(1, half)) + [0]:
            if k == 0:
                target, peer = ref.at[lax.rem(odd + half - 1, half), 1], sibling
            else:
                target, peer = ref.at[half - k, 0], lax.rem(me + 2 * k, n)
            copy = remote(
                ref.at[0, 0], target, send.at[min(k, 1)], recv.at[k], peer
            )
            copy.start()
            copies.append(copy)
        return copies

    def others(ref, first, parity):
        return ref.at[pl.ds(first, half - 1), parity]

    def arrived(ref, send, recv):
        return remote(others(ref, 1, 0), others(ref, 1, 0), send.at[1], recv.at[1], sibling)

    def small_piece(k):
        part = small.at[half - k, 0]
        return remote(part, part, small_send.at[1], small_recv.at[k], sibling)

    plane, last = me // 4, n // 4 - 1
    keys = [lax.rem(me - (n - 4 + odd + 2 * j) + n, n) // 2 for j in (0, 1)]

    def wait_last_plane():
        for key in keys:
            @pl.when(key > 0)
            def _(key=key):
                small_piece(key).wait_recv()

    def wait_other_planes():
        for k in range(1, half):
            @pl.when((keys[0] != k) & (keys[1] != k))
            def _(k=k):
                small_piece(k).wait_recv()

    def pass_on(ref, send, recv):
        copy = remote(others(ref, 1, 0), others(ref, odd, 1), send.at[2], recv.at[half], sibling)
        copy.start()
        return copy

    def wait_rest(copies, passed):
        copies[-1].wait_recv()
        passed.wait_recv()

    def wait_sent(ref, send, recv, copies, passed):
        arrived(ref, send, recv).wait_send()
        copies[-1].wait_send()
        passed.wait_send()

    small_copies = spread_own(small, small_send, small_recv)
    def big_copy(k):
        group = 0 if k == 0 else 1 + (k >= NEAR)
        if k == 0:
            target, peer = given.at[lax.rem(odd + half - 1, half), 1], sibling
        else:
            target, peer = given.at[half - k, 0], lax.rem(me + 2 * k, n)
        return remote(given.at[0, 0], target, big_send.at[group], big_recv.at[group], peer)

    def waits(k):
        facing = (k == half - 1) & (lax.rem(me // 2, 2) == 1)
        return (plane > 0) & (me // 2 + k >= n // 2) & jnp.logical_not(facing)

    def send_big(late):
        for k in range(1, half):
            @pl.when(waits(k) if late else jnp.logical_not(waits(k)))
            def _(k=k):
                big_copy(k).start()

    send_big(False)
    big_copies = [big_copy(0)]
    big_copies[0].start()
    groups = {1: (half - NEAR + 1, NEAR - 1), 2: (1, half - NEAR)}

    def big_arrived(group):
        part = given.at[pl.ds(*groups[group]), 0]
        return remote(part, part, big_send.at[group], big_recv.at[group], sibling)

    big_passed = []

    def pass_big(group):
        first, count = groups[group]
        big_arrived(group).wait_recv()
        copy = remote(
            given.at[pl.ds(first, count), 0], given.at[pl.ds(first - 1 + odd, count), 1],
            big_send.at[2 + group], big_recv.at[2 + group], sibling,
        )
        copy.start()
        big_passed.append(copy)


    for load in loads[5:]:
        load.wait()

    spread = ones_where(
        iota((256, 64), 1) == (iota((256, 64), 0) >> 7) * 32 + (iota((256, 64), 0) & 31)
    )
    taps = nt(spread, conv[...]).astype(bf16)
    shape = (256, 160)
    lead = (iota(shape, 1) >> 5) - ((iota(shape, 0) & 127) >> 5)
    pick = iota((64, 160), 0) == (iota((64, 160), 1) & 31)
    later = iota((64, 160), 0) == (iota((64, 160), 1) & 31) + 32
    band = jnp.where(lead == 0, nn(taps, ones_where(pick)), 0.0)
    band = jnp.where(lead == 1, nn(taps, ones_where(later)), band)
    band = jnp.where(iota(shape, 0) < 128, band, 0.5 * band).astype(bf16)
    shape = (384, 32)
    spread = ones_where(iota(shape, 1) == (iota(shape, 0) & 31))
    rows = nn(spread, mix[...])
    rows = jnp.where((iota((384, 96), 1) >> 5) == (iota((384, 96), 0) >> 7), rows, 0.0).astype(bf16)
    spread = ones_where((iota((96, 128), 0) & 31) == (iota((96, 128), 1) & 31))
    shape = (384, 128)
    mix_big[...] = jnp.where(
        ((iota(shape, 0) & 127) >> 5) == (iota(shape, 1) >> 5), nn(rows, spread), 0.0
    ).astype(bf16)
    columns = jnp.concatenate(
        [jnp.concatenate([start_proj[...]] * 4, axis=1), jnp.zeros((126, 128), f32)], axis=0
    ).T
    weight, bias = columns[0:32, 0:1], columns[0:32, 1:2]
    inputs[0:32, :] = jnp.broadcast_to(bias, (32, total)).astype(bf16)

    wait_last_plane()

    send_big(True)
    wait_other_planes()
    small_passed = pass_on(small, small_send, small_recv)

    wait_rest(small_copies, small_passed)

    by_lane = list(range(0, n, 2)) + list(range(1, n, 2))

    def across(lanes):
        whole = jnp.concatenate([small[k // 2, k % 2, :, lanes] for k in by_lane], axis=1)
        return jnp.where(iota((16, total), 0) < 10, whole, 0.0)

    high, middle, low = thirds(across(slice(0, SLOT)) * LOG2_E)
    left[...] = jnp.concatenate([high, middle, low, high, high, middle], axis=0)
    high, middle, low = thirds(across(slice(64, 64 + SLOT)))
    right[...] = jnp.concatenate([high, middle, high, low, middle, high], axis=0)

    numbers = jnp.concatenate([small[:, :, q, 48:64].reshape(n, 16) for q in range(3)], axis=1)
    numbers = jnp.concatenate([numbers[k : k + 1, :] for k in by_lane], axis=1).astype(jnp.int32)
    owner = (numbers * 1366) >> 16
    place = numbers - SLOT * owner
    owner = (owner - me + n) & (n - 1)
    high, low = halves(small[:, :, 8:16, :].reshape(8 * n, 128))
    found = jnp.concatenate([high, low], axis=1)

    def pick_steps(offset):
        onehot = ones_where(iota((128, total), 0) == place + offset)
        steps = nn(found, jnp.concatenate([onehot, onehot], axis=0))
        terms = [jnp.where(owner == k, steps[8 * k : 8 * k + 8, :], 0.0) for k in range(n)]
        while len(terms) > 1:
            terms = [a + b for a, b in zip(terms[::2], terms[1::2])]
        return terms[0]

    picked[0:8, :] = pick_steps(0)
    picked[8:16, :] = pick_steps(64)
    for t in range(STEPS):
        inputs[32 * t + 32 : 32 * t + 64, :] = (picked[t + 2 + 2 * (t // 6) : t + 3 + 2 * (t // 6), :] * weight + bias).astype(bf16)
    for b in range(3):
        terms = nn(band, inputs[128 * b : 128 * b + 160, :])
        gated = jnp.tanh(terms[:128, :]) * (0.5 * jnp.tanh(terms[128:, :]) + 0.5)
        hidden[128 * b : 128 * b + 128, :] = gated.astype(bf16)

    chunks = [slice(at, at + WIDE) for at in range(0, total, WIDE)]
    tiles = [slice(128 * b, 128 * b + 128) for b in range(3)]
    for cols in chunks:
        scores = tn(right[...], left[:, cols])
        top = jnp.maximum(jnp.max(scores, axis=0, keepdims=True), 0.0)
        terms = jnp.exp2(jnp.maximum(scores, 0.0) - top)
        weights[:, cols] = terms.astype(bf16)
        inverse = 1.0 / jnp.sum(terms, axis=0, keepdims=True)
        stats[0:1, cols] = top
        stats[1:2, cols] = inverse
    for cols in chunks:
        result = nn(hidden[...], weights[:, cols]) * stats[1:2, cols]
        diffused[:, cols] = result.astype(bf16)
    for rows in tiles:
        both = nn(mix_big[128:384, :], diffused[rows, :])
        mixed_one[rows, :] = both[:128, :]
        mixed_two[rows, :] = both[128:, :].astype(bf16)
        more = nn(mix_big[128:384, :], hidden[rows, :])
        ahead[rows, :] = (both[128:, :] + more[:128, :]).astype(bf16)
        twice[rows, :] = more[128:, :].astype(bf16)

    pass_big(1)
    for cols in chunks:
        result = nn(mixed_two[...], weights[:, cols]) * stats[1:2, cols]
        mixed_one[:, cols] = mixed_one[:, cols] + result

    own = slice(0, 128)
    for rows in tiles:
        summed = inputs[32 + rows.start : 160 + rows.start, own].astype(f32)
        summed = summed + nn(mix_big[0:128, :], hidden[rows, own]) + mixed_one[rows, own]
        layer_out[:, rows] = summed.T[0:SLOT, :].astype(bf16)
    scores = tn(right[:, own], left[...])[0:SLOT, :]
    shares = jnp.exp2(jnp.maximum(scores, 0.0) - stats[0:1, :]) * stats[1:2, :]
    shares_dst[...] = jnp.where(scores > 0.0, shares, 0.0)
    scores = tn(left[:, own], right[...])[0:SLOT, :]
    top = jnp.maximum(jnp.max(scores, axis=1, keepdims=True), 0.0)
    terms = jnp.exp2(jnp.maximum(scores, 0.0) - top)
    shares = terms * (1.0 / jnp.sum(terms, axis=1, keepdims=True))
    shares_src[...] = shares
    masked_src[...] = jnp.where(scores > 0.0, shares, 0.0)
    dots_src[...] = nn(given[0, 0], ahead[...])

    pass_big(2)

    def take(parity):
        cols = slice(SLOT * half * parity, SLOT * half * (parity + 1))
        part = given[:, parity].reshape(SLOT * half, 384).T
        grads[:, cols] = part
        part = part.astype(f32)
        stats[2:3, cols] = jnp.sum(part * mixed_one[:, cols], axis=0, keepdims=True)
        inputs[0:384, cols] = (part * stats[1:2, cols]).astype(bf16)

    def use(parity):
        cols = slice(SLOT * half * parity, SLOT * half * (parity + 1))
        dots_dst[:, cols] = tn(ahead[:, own], grads[:, cols])[0:SLOT, :]
        natural = given[:, parity].reshape(SLOT * half, 384)
        return sum(
            nn(jnp.concatenate([hidden[rows, cols], diffused[rows, cols]], axis=0), natural[:, rows])
            for rows in tiles
        )

    take(0)
    mixed_grad[...] = use(0)
    early = slice(0, SLOT * half)
    for cols in chunks:
        partial[:, cols] = nt(inputs[0:384, early], weights[cols, early])
    for copy in big_copies[-1:] + big_passed:
        copy.wait_recv()
    take(1)
    for cols in chunks:
        result = partial[:, cols] + nt(inputs[0:384, SLOT * half : total], weights[cols, SLOT * half : total])
        back[:, cols] = result.astype(bf16)
        stats[2:3, cols] = stats[2:3, cols] + jnp.sum(
            result * mixed_two[:, cols].astype(f32), axis=0, keepdims=True
        )

    mixed_grad[...] = mixed_grad[...] + use(1)
    wait_sent(small, small_send, small_recv, small_copies, small_passed)
    big_arrived(1).wait_send()
    big_arrived(2).wait_send()
    for copy in big_copies[-1:] + big_passed:
        copy.wait_send()


def finish_kernel(
    n, diffused, back, twice, left, right, stats, layer_out, shares_src, masked_src, shares_dst, dots_src, dots_dst, mixed_grad,
    layer_out_to, grad_src_to, grad_dst_to, grad_mix_to,
    grad_src, grad_dst, grad_mix, store_sem,
):
    stores = [
        pltpu.make_async_copy(source, target, store_sem.at[at])
        for at, (source, target) in enumerate(
            [
                (layer_out, layer_out_to), (grad_mix, grad_mix_to),
                (grad_src, grad_src_to), (grad_dst, grad_dst_to),
            ]
        )
    ]
    stores[0].start()
    tiles = [slice(128 * b, 128 * b + 128) for b in range(3)]
    own = slice(0, 128)

    def score_grad(value, stacked):
        high, low = halves(value)
        return nt(stacked, jnp.concatenate([high, low], axis=0))

    dots_to = dots_dst[...] + tn(twice[:, own], back[...])[0:SLOT, :] - stats[2:3, :]
    dots_from = dots_src[...] + tn(back[:, own], twice[...])[0:SLOT, :]
    delta = jnp.sum(shares_src[...] * dots_from, axis=1, keepdims=True)
    to = score_grad(shares_dst[...] * dots_to, left[0:48, :])
    source = score_grad(masked_src[...] * (dots_from - delta), right[0:64, :])
    again = sum(nt(diffused[rows, :], back[rows, :]) for rows in tiles)
    to = to[0:16, :] + to[16:32, :] + to[32:48, :]
    source = source[0:16, :] + source[16:32, :] + source[48:64, :]
    grad_dst[...] = (to[0:10, 0:SLOT] + to[0:10, SLOT : 2 * SLOT]) * (1.0 / LOG2_E)
    grad_src[...] = source[0:10, 0:SLOT] + source[0:10, SLOT : 2 * SLOT]
    mixed = [
        sum(block[32 * t : 32 * (t + 1), 32 * t : 32 * (t + 1)] for t in range(4))
        for block in (mixed_grad[0:128, :], mixed_grad[128:256, :], again)
    ]
    mixed = jnp.concatenate(mixed + [jnp.zeros((32, 32), f32)], axis=0)
    mixed = jnp.concatenate([mixed, jnp.zeros((128, 96), f32)], axis=1)
    grad_mix[...] = mixed.T[0:32, 0:96]
    for store in stores[1:]:
        store.start()
    for store in stores:
        store.wait()


def whole_in_kernel(
    series, starts, sensor_order, emb_src, emb_dst, start_proj, conv_weight, mix_weight, out_grad
):
    n = lax.axis_size("sensor")
    total = SLOT * n
    vmem = pl.BlockSpec(memory_space=pltpu.VMEM)
    anywhere = pl.BlockSpec(memory_space=pltpu.HBM)
    dma = pltpu.SemaphoreType.DMA
    wide = jax.ShapeDtypeStruct((384, total), bf16)
    strip = jax.ShapeDtypeStruct((SLOT, total), f32)
    stacked = jax.ShapeDtypeStruct((96, total), bf16)
    operands = (
        series.T, sensor_order.reshape(1, -1), emb_src, emb_dst, start_proj, conv_weight,
        mix_weight.T, out_grad,
    )
    operands = tuple(pltpu.with_memory_space_constraint(operand, pltpu.HBM) for operand in operands)
    staged = [operands[at] for at in (0, 1, 2, 3, 4, 5, 6)]
    held = pl.pallas_call(
        lambda *refs: gather_kernel(n, *refs),
        out_shape=(
            wide, wide, wide, stacked, stacked,
            jax.ShapeDtypeStruct((8, total), f32),
            jax.ShapeDtypeStruct((SLOT, 384), bf16),
            strip, strip, strip, strip, strip,
            jax.ShapeDtypeStruct((256, 128), f32),
        ),
        in_specs=[pl.BlockSpec(memory_space=pltpu.SMEM)] + [anywhere] * 8,
        out_specs=(vmem,) * 13,
        scratch_shapes=[pltpu.VMEM(operand.shape, operand.dtype) for operand in staged]
        + [
            pltpu.VMEM((n // 2, 2, 16, 128), f32),
            pltpu.VMEM((n // 2, 2, SLOT, 384), bf16),
            pltpu.VMEM((416, total), bf16),
            pltpu.VMEM((16, total), f32),
            pltpu.VMEM((total, total), bf16),
            pltpu.VMEM((384, total), f32),
            pltpu.VMEM((384, total), f32),
            pltpu.VMEM((384, total), bf16),
            pltpu.VMEM((384, total), bf16),
            pltpu.VMEM((384, total), bf16),
            pltpu.VMEM((384, total), bf16),
            pltpu.VMEM((384, 128), bf16),
            dma((8,)),
            dma((3,)),
            dma((n // 2 + 1,)),
            dma((5,)),
            dma((5,)),
        ],
        compiler_params=pltpu.CompilerParams(
            collective_id=0, has_side_effects=True, vmem_limit_bytes=32 * 2**20
        ),
    )(starts, *operands)
    outs = (
        jax.ShapeDtypeStruct((48, 384), bf16),
        jax.ShapeDtypeStruct((10, 48), f32),
        jax.ShapeDtypeStruct((10, 48), f32),
        jax.ShapeDtypeStruct((32, 96), f32),
    )
    layer_out, grad_src, grad_dst, grad_mix = pl.pallas_call(
        lambda *refs: finish_kernel(n, *refs),
        out_shape=outs,
        in_specs=[vmem] * 13,
        out_specs=(anywhere,) * 4,
        scratch_shapes=[pltpu.VMEM(out.shape, out.dtype) for out in outs[1:]] + [dma((4,))],
        compiler_params=pltpu.CompilerParams(vmem_limit_bytes=32 * 2**20),
    )(*held)
    return layer_out, grad_src, grad_dst, grad_mix.T


def layer_on_device(*operands):
    if lax.axis_size("sensor") == 16 and operands[2].shape[0] == 48:
        return whole_in_kernel(*operands)
    return per_device(*operands)


def solution(mesh):
    placed = (
        P(None, ("groups", "sensor")),
        P("groups"),
        P(("groups", "sensor")),
        P(None, ("groups", "sensor")),
        P(None, ("groups", "sensor")),
        P(),
        P(),
        P(),
        P(("groups", "sensor"), None),
    )
    return jax.shard_map(
        layer_on_device,
        mesh=mesh,
        in_specs=placed,
        out_specs=(
            P(("groups", "sensor"), None),
            P(None, ("groups", "sensor")),
            P(None, ("groups", "sensor")),
            P("groups", None),
        ),
        check_vma=False,
    )
```
